256 devices in a mesh: panel: 8 (over z), rows: 32 (over y, x, core).
Axes of the slice: x: 4, y: 4, z: 8, core: 2. Of those that a mesh axis runs over, the one named last changes fastest.
Arguments:
- rhs_diag: bfloat16 [8, 8192, 128], P(None, 'rows'), may hold values from -6 to 6
- rhs_tall: bfloat16 [8, 16384, 128], P('panel', 'rows'), may hold values from -6 to 6
- diag_inverse: bfloat16 [8, 1024, 1024], P('panel'), may hold values from -0.1875 to 0.1875
- coupling: bfloat16 [8, 8192, 1024], P('panel', 'rows'), may hold values from -0.09375 to 0.09375
- tall_blocks: bfloat16 [8, 128, 128, 1024], P('panel', 'rows'), may hold values from -0.125 to 0.125
- sparsity: int32 [128, 8], P('rows', 'panel'), may hold values 0 or 1
Outputs:
- solution: float32 [8, 8, 1024, 128], P('panel', None, 'rows')
- tall_residual: float32 [8, 16384, 128], P('panel', 'rows')
The draws below stay inside these ranges and needn't reach their ends.
All inputs are finite; a program needn't handle non-finite values. No bound on the sum of `sparsity` on one device may be relied on, other than what follows from the above.
Results may differ from the reference program's by a relative error of at most 0.0085.
Values may be sent and summed in bfloat16 or wider, within the bound.
No kernel may reach another device: no remote copies, remote signals or barrier semaphores. Data moves between devices by JAX's collectives and lax.ppermute only.
A program may use at most 64 MiB of HBM per device.

```python
import jax
import jax.numpy as jnp

W = 1024
BLK = 128
RHS = 128
PANELS = 8
BATCHES = 8
ORDER = 8192
NBLK = 128
TALL = 16384


def with_ends(entries, own_key, smallest, top_value):
    longest = entries.shape.index(max(entries.shape))
    spots = []
    for shift in (0, 1):
        where = [jax.random.randint(jax.random.fold_in(own_key, axis), (), 0, length) for axis, length in enumerate(entries.shape)]
        where[longest] = (where[longest] + shift) % entries.shape[longest]
        spots.append(tuple(where))
    return entries.at[spots[0]].set(smallest).at[spots[1]].set(top_value)


def block_scale(rng, shape, split, low, high):
    level = 1.0
    for position, shards_of in split:
        draws = jax.random.uniform(jax.random.fold_in(jax.random.fold_in(rng, 6), position), (shards_of,), jnp.float32, low / len(split), high / len(split))
        level = level * jnp.repeat(jnp.exp(draws), shape[position] // shards_of).reshape((-1,) + (1,) * (len(shape) - 1 - position))
    return level


def scatter_about(rng, dims, width, bound, pieces=(), kind=jnp.bfloat16):
    loudness = block_scale(rng, dims, pieces, -0.22, 0.18) if pieces else 1.0
    values = jax.random.normal(rng, dims, jnp.float32) * width * loudness
    return jnp.minimum(jnp.maximum(values, -bound), bound).astype(kind)


def setup_inputs(seed: int = 0) -> dict:
    key_of = jax.random.split(jax.random.key(seed), 7)
    rhs_diag = scatter_about(key_of[0], (BATCHES, ORDER, RHS), 1.0, 6.0, ((1, 32),))
    rhs_tall = scatter_about(key_of[1], (BATCHES, TALL, RHS), 1.0, 6.0, ((0, 8), (1, 32)))
    diag_inverse = scatter_about(key_of[2], (PANELS, W, W), W ** -0.5, 0.1875, ((0, 8),))
    coupling = scatter_about(key_of[3], (PANELS, ORDER, W), (4 * W) ** -0.5, 0.09375, ((0, 8), (1, 32)))
    tall_blocks = scatter_about(key_of[4], (PANELS, NBLK, BLK, W), (2 * W) ** -0.5, 0.125, ((0, 8), (1, 32)))
    sparsity = with_ends((jax.random.randint(key_of[5], (NBLK, PANELS), 0, 2) < 1).astype(jnp.int32), jax.random.fold_in(key_of[5], 1), 0, 1)
    return {"rhs_diag": rhs_diag, "rhs_tall": rhs_tall, "diag_inverse": diag_inverse, "coupling": coupling, "tall_blocks": tall_blocks, "sparsity": sparsity}


def reference(rhs_diag, rhs_tall, diag_inverse, coupling, tall_blocks, sparsity):
    row_panel = jnp.arange(ORDER, dtype=jnp.int32) // W
    block_mask = jnp.repeat(sparsity.astype(jnp.float32), BLK, axis=0)
    per_batch = []
    for batch_index in range(BATCHES):
        running = jnp.zeros((ORDER, RHS), jnp.float32)
        solved_list = []
        for column_panel in range(PANELS):
            lower = column_panel * W
            rhs_now = rhs_diag[batch_index, lower:lower + W].astype(jnp.float32)
            reduced = (rhs_now - running[lower:lower + W]).astype(jnp.bfloat16)
            solved = jnp.dot(diag_inverse[column_panel], reduced, preferred_element_type=jnp.float32)
            solved_list.append(solved)
            update = jnp.dot(coupling[column_panel], solved.astype(jnp.bfloat16), preferred_element_type=jnp.float32)
            running = running + jnp.where((row_panel > column_panel)[:, None], update, jnp.float32(0.0))
        per_batch.append(jnp.stack(solved_list))
    solution = jnp.stack(per_batch, axis=1)
    tall_sum = jnp.zeros((TALL, BATCHES * RHS), jnp.float32)
    for column_panel in range(PANELS):
        operand = jnp.transpose(solution[column_panel].astype(jnp.bfloat16), (1, 0, 2)).reshape(W, BATCHES * RHS)
        product = jnp.dot(tall_blocks[column_panel].reshape(TALL, W), operand, preferred_element_type=jnp.float32)
        tall_sum = tall_sum + product * block_mask[:, column_panel:column_panel + 1]
    tall_sum = jnp.transpose(tall_sum.reshape(TALL, BATCHES, RHS), (1, 0, 2))
    return solution, rhs_tall.astype(jnp.float32) - tall_sum
```

```python
import jax
import jax.numpy as jnp
from jax import lax
from jax.sharding import Mesh
from jax.sharding import PartitionSpec as P

F32 = jnp.float32
BF16 = jnp.bfloat16
ROWS = ("chip", "core")


def times(left, weight):
    return lax.dot_general(
        left, weight, (((1,), (1,)), ((), ())), preferred_element_type=F32
    )


def per_device(rhs_diag, rhs_tall, diag_inverse, coupling, tall_blocks, sparsity):
    z = lax.axis_index("panel")
    rows_index = lax.axis_index(ROWS)
    core = lax.axis_index("core")
    panels = lax.axis_size("panel")
    chips = lax.axis_size("chip")
    groups = lax.axis_size(ROWS)
    batches, rows_here, columns = rhs_diag.shape
    width = diag_inverse.shape[1]
    owners = width // rows_here
    share = batches * columns // groups
    parts = columns // share
    slice_rows = width // groups

    whole = lax.all_gather(coupling[0], ROWS).reshape(panels, width, width)

    pieces = rhs_diag.reshape(batches, rows_here, parts, share)
    pieces = pieces.transpose(0, 2, 3, 1).reshape(groups, share, rows_here)
    pieces = lax.all_to_all(pieces, ROWS, 0, 0, tiled=True)
    own = lax.dynamic_slice_in_dim(pieces, owners * z, owners, 0)
    own_rhs = own.transpose(1, 0, 2).reshape(share, width).astype(F32)

    inverse = diag_inverse[0]
    following = lax.dynamic_index_in_dim(
        whole, jnp.minimum(z + 1, panels - 1), 0, keepdims=False
    )

    def weight_of(index):
        return lax.dynamic_index_in_dim(
            whole, jnp.clip(index, 0, panels - 1), 0, keepdims=False
        )

    zero = jnp.zeros((share, width), F32)
    solved = jnp.zeros((share, width), BF16)
    near = zero
    even, odd = [zero, zero], [zero]
    for k in range(panels):
        reduced = (own_rhs - (near + even[k])).astype(BF16)
        fresh = times(reduced, inverse).astype(BF16)
        solved = jnp.where(z == k, fresh, solved)
        if k == panels - 1:
            break
        into_odd = odd[k]
        into_even = even[k + 1]
        near = lax.ppermute(times(fresh, following) + into_odd, "panel", [(k, k + 1)])
        senders = range(max(0, 2 * k - panels + 2), min(k, panels - 3) + 1)
        if k < panels - 2:
            far_odd = into_odd + times(solved, weight_of(2 * k + 1 - z))
            far_even = into_even + times(solved, weight_of(2 * k + 2 - z))
            both = jnp.stack([far_odd, far_even]).astype(BF16)
            both = lax.ppermute(both, "panel", [(s, s + 2) for s in senders])
            odd.append(both[0].astype(F32))
            even.append(both[1].astype(F32))
    mine = lax.all_to_all(
        jnp.broadcast_to(solved[None], (chips, share, width)), "chip", 0, 0, tiled=True
    )
    other = lax.ppermute(mine, "core", [(0, 1), (1, 0)])
    first = jnp.where(core == 0, mine, other)
    second = jnp.where(core == 0, other, mine)
    full = jnp.stack([first, second], 1).reshape(batches, columns, width)

    own_rows = lax.dynamic_slice_in_dim(full, rows_index * slice_rows, slice_rows, 2)
    solution_rows = own_rows.transpose(0, 2, 1).astype(F32)

    blocks, block_rows = tall_blocks.shape[1], tall_blocks.shape[2]
    tall = tall_blocks[0].reshape(blocks * block_rows, width)
    mask = jnp.repeat(sparsity[:, 0].astype(F32), block_rows)[:, None]
    terms = jnp.einsum("rw,bsw->brs", tall, full, preferred_element_type=F32) * mask
    summed = lax.psum_scatter(terms, "panel", scatter_dimension=0, tiled=True)
    return solution_rows[None], rhs_tall.astype(F32) - summed


def solution(mesh):
    panels, rows = mesh.devices.shape
    split = Mesh(mesh.devices.reshape(panels, rows // 2, 2), ("panel", "chip", "core"))
    placed = (
        P(None, ROWS, None),
        P("panel", ROWS, None),
        P("panel", None, None),
        P("panel", ROWS, None),
        P("panel", ROWS, None, None),
        P(ROWS, "panel"),
    )
    return jax.shard_map(
        per_device,
        mesh=split,
        in_specs=placed,
        out_specs=(P("panel", None, ROWS, None), P("panel", ROWS, None)),
        check_vma=False,
    )
```

```python
import jax
import jax.numpy as jnp
from jax import lax
from jax.experimental import pallas as pl
from jax.experimental.pallas import tpu as pltpu
from jax.sharding import Mesh
from jax.sharding import PartitionSpec as P

F32 = jnp.float32
BF16 = jnp.bfloat16
ROWS = ("chip", "core")
FAR_SENDS = {
    1: ((3, (0, 1)), (6, (0, 1))),
    2: ((4, (0, 1, 2)), (5, (0, 1, 2)), (7, (0,))),
    3: ((3, (2, 3)), (4, (3,))),
    4: ((3, (4,)),),
}


def times(left, weight):
    return lax.dot_general(
        left, weight, (((1,), (1,)), ((), ())), preferred_element_type=F32
    )


def later_body(
    place_ref, solved_ref, whole_ref, kept_ref, out_ref, weights, products, loaded, stored
):
    z = place_ref[0]
    count, panels = weights.shape[0], whole_ref.shape[0]

    def load(i):
        return pltpu.make_async_copy(whole_ref.at[z + 3 + i], weights.at[i], loaded.at[i])

    def store(i):
        return pltpu.make_async_copy(products.at[i], out_ref.at[i], stored.at[i])

    @pl.when(place_ref[1] == 1)
    def _():
        for i in range(count):

            @pl.when(z + 3 + i < panels)
            def _():
                load(i).start()

        for i in range(count):

            @pl.when(z + 3 + i < panels)
            def _():
                load(i).wait()
                products[i] = times(solved_ref[...], weights[i])
                store(i).start()

        for i in range(count):

            @pl.when(z + 3 + i < panels)
            def _():
                store(i).wait()


def later_products(z, turn, solved, whole, kept):
    count, share, width = kept.shape
    return pl.pallas_call(
        later_body,
        grid_spec=pltpu.PrefetchScalarGridSpec(
            num_scalar_prefetch=1,
            grid=(1,),
            in_specs=[
                pl.BlockSpec((share, width), lambda i, p: (0, 0)),
                pl.BlockSpec(memory_space=pl.ANY),
                pl.BlockSpec(memory_space=pl.ANY),
            ],
            out_specs=pl.BlockSpec(memory_space=pl.ANY),
            scratch_shapes=[
                pltpu.VMEM((count, width, width), BF16),
                pltpu.VMEM((count, share, width), F32),
                pltpu.SemaphoreType.DMA((count,)),
                pltpu.SemaphoreType.DMA((count,)),
            ],
        ),
        out_shape=jax.ShapeDtypeStruct(kept.shape, F32),
        input_output_aliases={3: 0},
        compiler_params=pltpu.CompilerParams(vmem_limit_bytes=16 * 2**20),
        name="later_products",
    )(jnp.stack([z, turn.astype(jnp.int32)]), solved, whole, kept)


def per_device(rhs_diag, rhs_tall, diag_inverse, coupling, tall_blocks, sparsity):
    z = lax.axis_index("panel")
    rows_index = lax.axis_index(ROWS)
    core = lax.axis_index("core")
    panels = lax.axis_size("panel")
    chips = lax.axis_size("chip")
    groups = lax.axis_size(ROWS)
    batches, rows_here, columns = rhs_diag.shape
    width = diag_inverse.shape[1]
    owners = width // rows_here
    share = batches * columns // groups
    parts = columns // share
    slice_rows = width // groups

    whole = lax.all_gather(coupling[0], ROWS).reshape(panels, width, width)

    pieces = rhs_diag.reshape(batches, rows_here, parts, share)
    pieces = pieces.transpose(0, 2, 3, 1).reshape(groups, share, rows_here)
    pieces = lax.all_to_all(pieces, ROWS, 0, 0, tiled=True)
    own = lax.dynamic_slice_in_dim(pieces, owners * z, owners, 0)
    own_rhs = own.transpose(1, 0, 2).reshape(share, width).astype(F32)

    inverse = diag_inverse[0]
    def ahead(distance):
        index = jnp.minimum(z + distance, panels - 1)
        return lax.dynamic_index_in_dim(whole, index, 0, keepdims=False)

    following, second = lax.optimization_barrier((ahead(1), ahead(2)))

    solved = jnp.zeros((share, width), BF16)
    kept = jnp.zeros((panels - 3, share, width), F32)
    arrivals = [[] for _ in range(panels)]

    def send(value, senders, distance):
        moved = lax.ppermute(value, "panel", [(s, s + distance) for s in senders])
        for s in senders:
            arrivals[s + distance].append(moved)

    for k in range(panels):
        earlier = sum(arrivals[k], jnp.zeros((share, width), F32))
        fresh = times((own_rhs - earlier).astype(BF16), inverse).astype(BF16)
        solved = jnp.where(z == k, fresh, solved)
        if k == panels - 1:
            break
        near = times(fresh, following)
        near, fresh = lax.optimization_barrier((near, fresh))
        send(near, [k], 1)
        if k < panels - 2:
            send(times(fresh, second), [k], 2)
        if k < panels - 3:
            kept = later_products(z, z == k, fresh, whole, kept)
        for distance, senders in FAR_SENDS.get(k, ()):
            send(kept[distance - 3], senders, distance)
    mine = lax.all_to_all(
        jnp.broadcast_to(solved[None], (chips, share, width)), "chip", 0, 0, tiled=True
    )
    other = lax.ppermute(mine, "core", [(0, 1), (1, 0)])
    first = jnp.where(core == 0, mine, other)
    second = jnp.where(core == 0, other, mine)
    full = jnp.stack([first, second], 1).reshape(batches, columns, width)

    own_rows = lax.dynamic_slice_in_dim(full, rows_index * slice_rows, slice_rows, 2)
    solution_rows = own_rows.transpose(0, 2, 1).astype(F32)

    blocks, block_rows = tall_blocks.shape[1], tall_blocks.shape[2]
    tall = tall_blocks[0].reshape(blocks * block_rows, width)
    mask = jnp.repeat(sparsity[:, 0].astype(F32), block_rows)[:, None]
    terms = jnp.einsum("rw,bsw->brs", tall, full, preferred_element_type=F32) * mask
    summed = lax.psum_scatter(terms, "panel", scatter_dimension=0, tiled=True)
    return solution_rows[None], rhs_tall.astype(F32) - summed


def solution(mesh):
    panels, rows = mesh.devices.shape
    split = Mesh(mesh.devices.reshape(panels, rows // 2, 2), ("panel", "chip", "core"))
    placed = (
        P(None, ROWS, None),
        P("panel", ROWS, None),
        P("panel", None, None),
        P("panel", ROWS, None),
        P("panel", ROWS, None, None),
        P(ROWS, "panel"),
    )
    return jax.shard_map(
        per_device,
        mesh=split,
        in_specs=placed,
        out_specs=(P("panel", None, ROWS, None), P("panel", ROWS, None)),
        check_vma=False,
    )
```

```python
import jax
import jax.numpy as jnp
from jax import lax
from jax.experimental import pallas as pl
from jax.experimental.pallas import tpu as pltpu
from jax.sharding import Mesh
from jax.sharding import PartitionSpec as P

F32 = jnp.float32
BF16 = jnp.bfloat16
ROWS = ("chip", "core")
FAR_SENDS = {
    1: ((3, (0, 1)),),
    2: ((4, (0, 1, 2)),),
    3: ((3, (2, 3)), (5, (0, 1, 2))),
    4: ((4, (3,)), (6, (0, 1))),
    5: ((3, (4,)), (7, (0,))),
}


def times(left, weight):
    return lax.dot_general(
        left, weight, (((1,), (1,)), ((), ())), preferred_element_type=F32
    )


def later_body(
    place_ref, solved_ref, whole_ref, kept_ref, out_ref, weights, products, loaded, stored
):
    z = place_ref[0]
    count, panels = weights.shape[0], whole_ref.shape[0]

    def load(i):
        return pltpu.make_async_copy(whole_ref.at[z + 3 + i], weights.at[i], loaded.at[i])

    def store(i):
        return pltpu.make_async_copy(products.at[i], out_ref.at[i], stored.at[i])

    @pl.when(place_ref[1] == 1)
    def _():
        valid = jnp.minimum(count, panels - 3 - z)
        lax.fori_loop(0, valid, lambda i, _: load(i).start(), None)

        def multiply(i, _):
            load(i).wait()
            products[i] = times(solved_ref[...], weights[i]).astype(BF16)
            store(i).start()

        lax.fori_loop(0, valid, multiply, None)
        lax.fori_loop(0, valid, lambda i, _: store(i).wait(), None)


def later_products(z, turn, solved, whole, kept):
    count, share, width = kept.shape
    return pl.pallas_call(
        later_body,
        grid_spec=pltpu.PrefetchScalarGridSpec(
            num_scalar_prefetch=1,
            grid=(1,),
            in_specs=[
                pl.BlockSpec((share, width), lambda i, p: (0, 0)),
                pl.BlockSpec(memory_space=pl.ANY),
                pl.BlockSpec(memory_space=pl.ANY),
            ],
            out_specs=pl.BlockSpec(memory_space=pl.ANY),
            scratch_shapes=[
                pltpu.VMEM((count, width, width), BF16),
                pltpu.VMEM((count, share, width), BF16),
                pltpu.SemaphoreType.DMA((count,)),
                pltpu.SemaphoreType.DMA((count,)),
            ],
        ),
        out_shape=jax.ShapeDtypeStruct(kept.shape, BF16),
        input_output_aliases={3: 0},
        compiler_params=pltpu.CompilerParams(vmem_limit_bytes=16 * 2**20),
        name="later_products",
    )(jnp.stack([z, turn.astype(jnp.int32)]), solved, whole, kept)


def per_device(rhs_diag, rhs_tall, diag_inverse, coupling, tall_blocks, sparsity):
    z = lax.axis_index("panel")
    rows_index = lax.axis_index(ROWS)
    core = lax.axis_index("core")
    panels = lax.axis_size("panel")
    chips = lax.axis_size("chip")
    groups = lax.axis_size(ROWS)
    batches, rows_here, columns = rhs_diag.shape
    width = diag_inverse.shape[1]
    owners = width // rows_here
    share = batches * columns // groups
    parts = columns // share
    slice_rows = width // groups

    whole = lax.all_gather(coupling[0], ROWS).reshape(panels, width, width)

    pieces = rhs_diag.reshape(batches, rows_here, parts, share)
    pieces = pieces.transpose(0, 2, 3, 1).reshape(groups, share, rows_here)
    pieces = lax.all_to_all(pieces, ROWS, 0, 0, tiled=True)
    own = lax.dynamic_slice_in_dim(pieces, owners * z, owners, 0)
    own_rhs = own.transpose(1, 0, 2).reshape(share, width).astype(F32)

    inverse = diag_inverse[0]
    def ahead(distance):
        index = jnp.minimum(z + distance, panels - 1)
        return lax.dynamic_index_in_dim(whole, index, 0, keepdims=False)

    following, second = lax.optimization_barrier((ahead(1), ahead(2)))

    solved = jnp.zeros((share, width), BF16)
    kept = jnp.zeros((panels - 3, share, width), BF16)
    arrivals = [[] for _ in range(panels)]

    def send(value, senders, distance):
        moved = lax.ppermute(value, "panel", [(s, s + distance) for s in senders])
        for s in senders:
            arrivals[s + distance].append(moved.astype(F32))

    for k in range(panels):
        earlier = sum(arrivals[k], jnp.zeros((share, width), F32))
        fresh = times((own_rhs - earlier).astype(BF16), inverse).astype(BF16)
        solved = jnp.where(z == k, fresh, solved)
        if k == panels - 1:
            break
        near = times(fresh, following).astype(BF16)
        near, fresh = lax.optimization_barrier((near, fresh))
        send(near, [k], 1)
        if k < panels - 2:
            send(times(fresh, second).astype(BF16), [k], 2)
        if k < panels - 3:
            kept = later_products(z, z == k, fresh, whole, kept)
        for distance, senders in FAR_SENDS.get(k, ()):
            send(kept[distance - 3], senders, distance)
    mine = lax.all_to_all(
        jnp.broadcast_to(solved[None], (chips, share, width)), "chip", 0, 0, tiled=True
    )
    other = lax.ppermute(mine, "core", [(0, 1), (1, 0)])
    sources = lax.broadcasted_iota(jnp.int32, (1, 2, 1, 1), 1)
    full = jnp.where(sources == core, mine[:, None], other[:, None])
    full = full.reshape(batches, columns, width)

    own_rows = lax.dynamic_slice_in_dim(full, rows_index * slice_rows, slice_rows, 2)
    solution_rows = own_rows.transpose(0, 2, 1).astype(F32)

    blocks, block_rows = tall_blocks.shape[1], tall_blocks.shape[2]
    tall = tall_blocks[0].reshape(blocks * block_rows, width)
    mask = jnp.repeat(sparsity[:, 0].astype(F32), block_rows)[:, None]

    def product(batch):
        term = times(tall, lax.dynamic_index_in_dim(full, batch, 0, keepdims=False))
        return term * mask

    summed = jnp.zeros((blocks * block_rows, columns), F32)
    for distance in sorted(range(1, panels), key=lambda d: abs(2 * d - panels)):
        term = product(lax.rem(z + distance, panels)).astype(BF16)
        route = [(s, (s + distance) % panels) for s in range(panels)]
        summed = summed + lax.ppermute(term, "panel", route).astype(F32)
    summed = summed + product(z)
    return solution_rows[None], rhs_tall.astype(F32) - summed[None]


def solution(mesh):
    panels, rows = mesh.devices.shape
    split = Mesh(mesh.devices.reshape(panels, rows // 2, 2), ("panel", "chip", "core"))
    placed = (
        P(None, ROWS, None),
        P("panel", ROWS, None),
        P("panel", None, None),
        P("panel", ROWS, None),
        P("panel", ROWS, None, None),
        P(ROWS, "panel"),
    )
    return jax.shard_map(
        per_device,
        mesh=split,
        in_specs=placed,
        out_specs=(P("panel", None, ROWS, None), P("panel", ROWS, None)),
        check_vma=False,
    )
```

```python
import jax
import jax.numpy as jnp
from jax import lax
from jax.experimental import pallas as pl
from jax.experimental.pallas import tpu as pltpu
from jax.sharding import Mesh
from jax.sharding import PartitionSpec as P

F32 = jnp.float32
BF16 = jnp.bfloat16
ROWS = ("chip", "core")
FAR_SENDS = {
    2: ((4, (0, 1)),),
    3: ((5, (0, 1, 2)),),
    4: ((4, (2, 3)), (6, (0, 1))),
    5: ((7, (0,)),),
}


def times(left, weight):
    return lax.dot_general(
        left, weight, (((1,), (1,)), ((), ())), preferred_element_type=F32
    )


def later_body(
    place_ref, solved_ref, whole_ref, kept_ref, out_ref, weights, products, loaded, stored
):
    z = place_ref[0]
    count, panels = weights.shape[0], whole_ref.shape[0]

    def load(i):
        return pltpu.make_async_copy(whole_ref.at[z + 4 + i], weights.at[i], loaded.at[i])

    def store(i):
        return pltpu.make_async_copy(products.at[i], out_ref.at[i], stored.at[i])

    @pl.when(place_ref[1] == 1)
    def _():
        valid = jnp.minimum(count, panels - 4 - z)
        lax.fori_loop(0, valid, lambda i, _: load(i).start(), None)

        def multiply(i, _):
            load(i).wait()
            products[i] = times(solved_ref[...], weights[i]).astype(BF16)
            store(i).start()

        lax.fori_loop(0, valid, multiply, None)
        lax.fori_loop(0, valid, lambda i, _: store(i).wait(), None)


def later_products(z, turn, solved, whole, kept):
    count, share, width = kept.shape
    return pl.pallas_call(
        later_body,
        grid_spec=pltpu.PrefetchScalarGridSpec(
            num_scalar_prefetch=1,
            grid=(1,),
            in_specs=[
                pl.BlockSpec((share, width), lambda i, p: (0, 0)),
                pl.BlockSpec(memory_space=pl.ANY),
                pl.BlockSpec(memory_space=pl.ANY),
            ],
            out_specs=pl.BlockSpec(memory_space=pl.ANY),
            scratch_shapes=[
                pltpu.VMEM((count, width, width), BF16),
                pltpu.VMEM((count, share, width), BF16),
                pltpu.SemaphoreType.DMA((count,)),
                pltpu.SemaphoreType.DMA((count,)),
            ],
        ),
        out_shape=jax.ShapeDtypeStruct(kept.shape, BF16),
        input_output_aliases={3: 0},
        compiler_params=pltpu.CompilerParams(vmem_limit_bytes=48 * 2**20),
        cost_estimate=pl.CostEstimate(
            flops=2 * count * share * width * width,
            bytes_accessed=2 * count * width * width,
            transcendentals=0,
        ),
        name="later_products",
    )(jnp.stack([z, turn.astype(jnp.int32)]), solved, whole, kept)


def per_device(rhs_diag, rhs_tall, diag_inverse, coupling, tall_blocks, sparsity):
    z = lax.axis_index("panel")
    rows_index = lax.axis_index(ROWS)
    core = lax.axis_index("core")
    panels = lax.axis_size("panel")
    chips = lax.axis_size("chip")
    groups = lax.axis_size(ROWS)
    batches, rows_here, columns = rhs_diag.shape
    width = diag_inverse.shape[1]
    owners = width // rows_here
    share = batches * columns // groups
    parts = columns // share
    slice_rows = width // groups

    whole = lax.all_gather(coupling[0], ROWS).reshape(panels, width, width)

    pieces = rhs_diag.reshape(batches, rows_here, parts, share)
    pieces = pieces.transpose(0, 2, 3, 1).reshape(groups, share, rows_here)
    pieces = lax.all_to_all(pieces, ROWS, 0, 0, tiled=True)
    own = lax.dynamic_slice_in_dim(pieces, owners * z, owners, 0)
    own_rhs = own.transpose(1, 0, 2).reshape(share, width).astype(F32)

    def swap(value):
        return lax.ppermute(value, "core", [(0, 1), (1, 0)])

    tall = tall_blocks[0] * sparsity[:, 0].astype(BF16)[:, None, None]
    tall = tall.reshape(-1, width)
    tall_rows = tall.shape[0]
    both_tall = jnp.concatenate([tall, swap(tall)])
    own_rhs, both_tall = lax.optimization_barrier((own_rhs, both_tall))

    inverse = diag_inverse[0]
    def ahead(distance):
        index = jnp.minimum(z + distance, panels - 1)
        return lax.dynamic_index_in_dim(whole, index, 0, keepdims=False)

    following, second, third = lax.optimization_barrier((ahead(1), ahead(2), ahead(3)))

    solved = jnp.zeros((share, width), BF16)
    kept = jnp.zeros((panels - 4, share, width), BF16)
    arrivals = [[] for _ in range(panels)]

    def send(value, senders, distance):
        moved = lax.ppermute(value, "panel", [(s, s + distance) for s in senders])
        for s in senders:
            arrivals[s + distance].append(moved.astype(F32))

    for k in range(panels):
        earlier = sum(arrivals[k], jnp.zeros((share, width), F32))
        fresh = times((own_rhs - earlier).astype(BF16), inverse).astype(BF16)
        solved = jnp.where(z == k, fresh, solved)
        if k == panels - 1:
            break
        if k > 0:
            fresh, previous = lax.optimization_barrier((fresh, previous))
        near = times(fresh, following).astype(BF16)
        near, fresh = lax.optimization_barrier((near, fresh))
        send(near, [k], 1)
        if k < panels - 2:
            send(times(fresh, second).astype(BF16), [k], 2)
        if k < panels - 3:
            send(times(fresh, third).astype(BF16), [k], 3)
        if 0 < k < panels - 3:
            kept = later_products(z, z == k - 1, previous, whole, kept)
        previous = fresh
        for distance, senders in FAR_SENDS.get(k, ()):
            send(kept[distance - 4], senders, distance)
    mine = lax.all_to_all(
        jnp.broadcast_to(solved[None], (chips, share, width)), "chip", 0, 0, tiled=True
    )
    products = times(mine.reshape(-1, width), both_tall).astype(BF16)
    products = products.reshape(batches, -1, 2 * tall_rows)

    def part(batch):
        return lax.dynamic_index_in_dim(products, batch, 0, keepdims=False)

    summed = part(z).astype(F32)
    for distance in sorted(range(1, panels), key=lambda d: -abs(2 * d - panels)):
        route = [(s, (s + distance) % panels) for s in range(panels)]
        moved = lax.ppermute(part(lax.rem(z + distance, panels)), "panel", route)
        summed = summed + moved.astype(F32)

    def in_order(own, other):
        lead, rows = own.shape[:-2], own.shape[-1]
        own = own.reshape(*lead, -1, 1, share, rows)
        other = other.reshape(*lead, -1, 1, share, rows)
        sides = lax.broadcasted_iota(jnp.int32, (2, 1, 1), 0)
        whole_row = jnp.where(sides == core, own, other).reshape(*lead, columns, rows)
        return jnp.swapaxes(whole_row, -1, -2)

    def rows_of(index):
        rows = lax.dynamic_slice_in_dim(mine, index * slice_rows, slice_rows, 2)
        return rows.reshape(batches, -1, slice_rows)

    other_rows = swap(rows_of(rows_index + 1 - 2 * core))
    solution_rows = in_order(rows_of(rows_index), other_rows).astype(F32)

    tall_sum = in_order(summed[:, :tall_rows], swap(summed[:, tall_rows:]))
    return solution_rows[None], rhs_tall.astype(F32) - tall_sum[None]


def solution(mesh):
    panels, rows = mesh.devices.shape
    split = Mesh(mesh.devices.reshape(panels, rows // 2, 2), ("panel", "chip", "core"))
    placed = (
        P(None, ROWS, None),
        P("panel", ROWS, None),
        P("panel", None, None),
        P("panel", ROWS, None),
        P("panel", ROWS, None, None),
        P(ROWS, "panel"),
    )
    return jax.shard_map(
        per_device,
        mesh=split,
        in_specs=placed,
        out_specs=(P("panel", None, ROWS, None), P("panel", ROWS, None)),
        check_vma=False,
    )
```

```python
import jax
import jax.numpy as jnp
from jax import lax
from jax.experimental import pallas as pl
from jax.experimental.pallas import tpu as pltpu
from jax.sharding import Mesh
from jax.sharding import PartitionSpec as P

F32 = jnp.float32
BF16 = jnp.bfloat16
ROWS = ("chip", "core")
FAR_SENDS = {
    2: ((4, (0, 1)),),
    3: ((5, (0, 1, 2)),),
    4: ((4, (2, 3)), (6, (0, 1))),
    5: ((7, (0,)),),
}


def times(left, weight):
    return lax.dot_general(
        left, weight, (((1,), (1,)), ((), ())), preferred_element_type=F32
    )


def later_body(
    place_ref, solved_ref, whole_ref, kept_ref, out_ref, weights, products, loaded, stored
):
    z = place_ref[0]
    count, panels = weights.shape[0], whole_ref.shape[0]

    def load(i):
        return pltpu.make_async_copy(whole_ref.at[z + 4 + i], weights.at[i], loaded.at[i])

    def store(i):
        return pltpu.make_async_copy(products.at[i], out_ref.at[i], stored.at[i])

    @pl.when(place_ref[1] == 1)
    def _():
        valid = jnp.minimum(count, panels - 4 - z)
        lax.fori_loop(0, valid, lambda i, _: load(i).start(), None)

        def multiply(i, _):
            load(i).wait()
            products[i] = times(solved_ref[...], weights[i]).astype(BF16)
            store(i).start()

        lax.fori_loop(0, valid, multiply, None)
        lax.fori_loop(0, valid, lambda i, _: store(i).wait(), None)


def later_products(z, turn, solved, whole, kept):
    count, share, width = kept.shape
    return pl.pallas_call(
        later_body,
        grid_spec=pltpu.PrefetchScalarGridSpec(
            num_scalar_prefetch=1,
            grid=(1,),
            in_specs=[
                pl.BlockSpec((share, width), lambda i, p: (0, 0)),
                pl.BlockSpec(memory_space=pl.ANY),
                pl.BlockSpec(memory_space=pl.ANY),
            ],
            out_specs=pl.BlockSpec(memory_space=pl.ANY),
            scratch_shapes=[
                pltpu.VMEM((count, width, width), BF16),
                pltpu.VMEM((count, share, width), BF16),
                pltpu.SemaphoreType.DMA((count,)),
                pltpu.SemaphoreType.DMA((count,)),
            ],
        ),
        out_shape=jax.ShapeDtypeStruct(kept.shape, BF16),
        input_output_aliases={3: 0},
        compiler_params=pltpu.CompilerParams(vmem_limit_bytes=48 * 2**20),
        cost_estimate=pl.CostEstimate(
            flops=2 * count * share * width * width,
            bytes_accessed=2 * count * width * width,
            transcendentals=0,
        ),
        name="later_products",
    )(jnp.stack([z, turn.astype(jnp.int32)]), solved, whole, kept)


def next_body(place_ref, solved_ref, whole_ref, *refs):
    *outs, weights, loaded = refs
    z, panels = place_ref[0], whole_ref.shape[0]

    def load(i):
        return pltpu.make_async_copy(whole_ref.at[z + 2 + i], weights.at[i], loaded.at[i])

    @pl.when(place_ref[1] == 1)
    def _():
        for i in range(len(outs)):

            @pl.when(z + 2 + i < panels)
            def _():
                load(i).start()

        for i in range(len(outs)):

            @pl.when(z + 2 + i < panels)
            def _():
                load(i).wait()
                outs[i][...] = times(solved_ref[...], weights[i]).astype(BF16)


def next_products(z, turn, solved, whole):
    share, width = solved.shape
    one = pl.BlockSpec((share, width), lambda i, p: (0, 0))
    return pl.pallas_call(
        next_body,
        grid_spec=pltpu.PrefetchScalarGridSpec(
            num_scalar_prefetch=1,
            grid=(1,),
            in_specs=[one, pl.BlockSpec(memory_space=pl.ANY)],
            out_specs=[one, one],
            scratch_shapes=[
                pltpu.VMEM((2, width, width), BF16),
                pltpu.SemaphoreType.DMA((2,)),
            ],
        ),
        out_shape=[jax.ShapeDtypeStruct((share, width), BF16)] * 2,
        compiler_params=pltpu.CompilerParams(vmem_limit_bytes=48 * 2**20),
        name="next_products",
    )(jnp.stack([z, turn.astype(jnp.int32)]), solved, whole)


def per_device(rhs_diag, rhs_tall, diag_inverse, coupling, tall_blocks, sparsity):
    z = lax.axis_index("panel")
    rows_index = lax.axis_index(ROWS)
    core = lax.axis_index("core")
    panels = lax.axis_size("panel")
    chips = lax.axis_size("chip")
    groups = lax.axis_size(ROWS)
    batches, rows_here, columns = rhs_diag.shape
    width = diag_inverse.shape[1]
    owners = width // rows_here
    share = batches * columns // groups
    parts = columns // share
    slice_rows = width // groups

    whole = lax.all_gather(coupling[0], ROWS).reshape(panels, width, width)

    pieces = rhs_diag.reshape(batches, rows_here, parts, share)
    pieces = pieces.transpose(0, 2, 3, 1).reshape(groups, share, rows_here)
    pieces = lax.all_to_all(pieces, ROWS, 0, 0, tiled=True)
    own = lax.dynamic_slice_in_dim(pieces, owners * z, owners, 0)
    own_rhs = own.transpose(1, 0, 2).reshape(share, width).astype(F32)

    def swap(value):
        return lax.ppermute(value, "core", [(0, 1), (1, 0)])

    tall = tall_blocks[0] * sparsity[:, 0].astype(BF16)[:, None, None]
    tall = tall.reshape(-1, width)
    tall_rows = tall.shape[0]
    both_tall = jnp.concatenate([tall, swap(tall)])
    own_rhs, both_tall = lax.optimization_barrier((own_rhs, both_tall))

    inverse = diag_inverse[0]
    def ahead(distance):
        index = jnp.minimum(z + distance, panels - 1)
        return lax.dynamic_index_in_dim(whole, index, 0, keepdims=False)

    following = lax.optimization_barrier(ahead(1))

    solved = jnp.zeros((share, width), BF16)
    kept = jnp.zeros((panels - 4, share, width), BF16)
    arrivals = [[] for _ in range(panels)]

    def send(value, senders, distance):
        moved = lax.ppermute(value, "panel", [(s, s + distance) for s in senders])
        for s in senders:
            arrivals[s + distance].append(moved.astype(F32))

    for k in range(panels):
        earlier = sum(arrivals[k], jnp.zeros((share, width), F32))
        fresh = times((own_rhs - earlier).astype(BF16), inverse).astype(BF16)
        solved = jnp.where(z == k, fresh, solved)
        if k == panels - 1:
            break
        if k > 0:
            fresh, previous = lax.optimization_barrier((fresh, previous))
        near = times(fresh, following).astype(BF16)
        near, fresh = lax.optimization_barrier((near, fresh))
        send(near, [k], 1)
        if k < panels - 2:
            after = next_products(z, z == k, fresh, whole)
            send(after[0], [k], 2)
        if k < panels - 3:
            send(after[1], [k], 3)
        if 0 < k < panels - 3:
            kept = later_products(z, z == k - 1, previous, whole, kept)
        previous = fresh
        for distance, senders in FAR_SENDS.get(k, ()):
            send(kept[distance - 4], senders, distance)
    mine = lax.all_to_all(
        jnp.broadcast_to(solved[None], (chips, share, width)), "chip", 0, 0, tiled=True
    )
    products = times(mine.reshape(-1, width), both_tall).astype(BF16)
    products = products.reshape(batches, -1, 2 * tall_rows)

    def part(batch):
        return lax.dynamic_index_in_dim(products, batch, 0, keepdims=False)

    summed = part(z).astype(F32)
    for distance in sorted(range(1, panels), key=lambda d: -abs(2 * d - panels)):
        route = [(s, (s + distance) % panels) for s in range(panels)]
        moved = lax.ppermute(part(lax.rem(z + distance, panels)), "panel", route)
        summed = summed + moved.astype(F32)

    def in_order(own, other):
        lead, rows = own.shape[:-2], own.shape[-1]
        own = own.reshape(*lead, -1, 1, share, rows)
        other = other.reshape(*lead, -1, 1, share, rows)
        sides = lax.broadcasted_iota(jnp.int32, (2, 1, 1), 0)
        whole_row = jnp.where(sides == core, own, other).reshape(*lead, columns, rows)
        return jnp.swapaxes(whole_row, -1, -2)

    def rows_of(index):
        rows = lax.dynamic_slice_in_dim(mine, index * slice_rows, slice_rows, 2)
        return rows.reshape(batches, -1, slice_rows)

    other_rows = swap(rows_of(rows_index + 1 - 2 * core))
    solution_rows = in_order(rows_of(rows_index), other_rows).astype(F32)

    tall_sum = in_order(summed[:, :tall_rows], swap(summed[:, tall_rows:]))
    return solution_rows[None], rhs_tall.astype(F32) - tall_sum[None]


def solution(mesh):
    panels, rows = mesh.devices.shape
    split = Mesh(mesh.devices.reshape(panels, rows // 2, 2), ("panel", "chip", "core"))
    placed = (
        P(None, ROWS, None),
        P("panel", ROWS, None),
        P("panel", None, None),
        P("panel", ROWS, None),
        P("panel", ROWS, None, None),
        P(ROWS, "panel"),
    )
    return jax.shard_map(
        per_device,
        mesh=split,
        in_specs=placed,
        out_specs=(P("panel", None, ROWS, None), P("panel", ROWS, None)),
        check_vma=False,
    )
```

```python
import jax
import jax.numpy as jnp
from jax import lax
from jax.experimental import pallas as pl
from jax.experimental.pallas import tpu as pltpu
from jax.sharding import Mesh
from jax.sharding import PartitionSpec as P

F32 = jnp.float32
BF16 = jnp.bfloat16
ROWS = ("chip", "core")
FAR_SENDS = {
    2: ((4, (0, 1)),),
    3: ((5, (0, 1, 2)),),
    4: ((4, (2, 3)), (6, (0, 1))),
    5: ((7, (0,)),),
}


def times(left, weight):
    return lax.dot_general(
        left, weight, (((1,), (1,)), ((), ())), preferred_element_type=F32
    )


def later_body(
    place_ref, solved_ref, whole_ref, kept_ref, out_ref, weights, products, loaded, stored
):
    z = place_ref[0]
    count, panels = weights.shape[0], whole_ref.shape[0]

    def load(i):
        return pltpu.make_async_copy(whole_ref.at[z + 4 + i], weights.at[i], loaded.at[i])

    def store(i):
        return pltpu.make_async_copy(products.at[i], out_ref.at[i], stored.at[i])

    @pl.when(place_ref[1] == 1)
    def _():
        valid = jnp.minimum(count, panels - 4 - z)
        lax.fori_loop(0, valid, lambda i, _: load(i).start(), None)

        def multiply(i, _):
            load(i).wait()
            products[i] = times(solved_ref[...], weights[i]).astype(BF16)
            store(i).start()

        lax.fori_loop(0, valid, multiply, None)
        lax.fori_loop(0, valid, lambda i, _: store(i).wait(), None)


def next_body(place_ref, solved_ref, whole_ref, *refs):
    *outs, weights, loaded = refs
    z, panels = place_ref[0], whole_ref.shape[0]

    def load(i):
        return pltpu.make_async_copy(whole_ref.at[z + 2 + i], weights.at[i], loaded.at[i])

    @pl.when(place_ref[2] == 1)
    def _():
        for i in range(len(outs)):

            @pl.when(z + 2 + i < panels)
            def _():
                load(i).start()

        for i in range(len(outs)):

            @pl.when(z + 2 + i < panels)
            def _():
                load(i).wait()
                outs[i][...] = times(solved_ref[...], weights[i]).astype(BF16)


def stage_body(place_ref, fresh_ref, previous_ref, whole_ref, kept_ref, *refs):
    next_a, next_b, out_ref, weights, products, loaded, stored, near_loaded = refs
    next_body(place_ref, fresh_ref, whole_ref, next_a, next_b, weights, near_loaded)
    later_body(
        place_ref, previous_ref, whole_ref, kept_ref, out_ref, weights, products, loaded, stored
    )


def stage_products(z, stage, fresh, previous, whole, kept):
    count, share, width = kept.shape
    one = pl.BlockSpec((share, width), lambda i, p: (0, 0))
    place = jnp.stack([z, z == stage - 1, z == stage]).astype(jnp.int32)
    part = jax.ShapeDtypeStruct((share, width), BF16)
    return pl.pallas_call(
        stage_body,
        grid_spec=pltpu.PrefetchScalarGridSpec(
            num_scalar_prefetch=1,
            grid=(1,),
            in_specs=[one, one] + [pl.BlockSpec(memory_space=pl.ANY)] * 2,
            out_specs=[one, one, pl.BlockSpec(memory_space=pl.ANY)],
            scratch_shapes=[
                pltpu.VMEM((count, width, width), BF16),
                pltpu.VMEM((count, share, width), BF16),
                pltpu.SemaphoreType.DMA((count,)),
                pltpu.SemaphoreType.DMA((count,)),
                pltpu.SemaphoreType.DMA((2,)),
            ],
        ),
        out_shape=[part, part, jax.ShapeDtypeStruct(kept.shape, BF16)],
        input_output_aliases={4: 2},
        compiler_params=pltpu.CompilerParams(vmem_limit_bytes=48 * 2**20),
        name="stage_products",
    )(place, fresh, previous, whole, kept)


def per_device(rhs_diag, rhs_tall, diag_inverse, coupling, tall_blocks, sparsity):
    z = lax.axis_index("panel")
    rows_index = lax.axis_index(ROWS)
    core = lax.axis_index("core")
    panels = lax.axis_size("panel")
    chips = lax.axis_size("chip")
    groups = lax.axis_size(ROWS)
    batches, rows_here, columns = rhs_diag.shape
    width = diag_inverse.shape[1]
    owners = width // rows_here
    share = batches * columns // groups
    parts = columns // share
    slice_rows = width // groups

    whole = lax.all_gather(coupling[0], ROWS).reshape(panels, width, width)

    pieces = rhs_diag.reshape(batches, rows_here, parts, share)
    pieces = pieces.transpose(0, 2, 3, 1).reshape(groups, share, rows_here)
    pieces = lax.all_to_all(pieces, ROWS, 0, 0, tiled=True)
    own = lax.dynamic_slice_in_dim(pieces, owners * z, owners, 0)
    own_rhs = own.transpose(1, 0, 2).reshape(share, width).astype(F32)

    def swap(value):
        return lax.ppermute(value, "core", [(0, 1), (1, 0)])

    tall = tall_blocks[0] * sparsity[:, 0].astype(BF16)[:, None, None]
    tall = tall.reshape(-1, width)
    tall_rows = tall.shape[0]
    both_tall = jnp.concatenate([tall, swap(tall)])
    own_rhs, both_tall = lax.optimization_barrier((own_rhs, both_tall))

    inverse = diag_inverse[0]
    def ahead(distance):
        index = jnp.minimum(z + distance, panels - 1)
        return lax.dynamic_index_in_dim(whole, index, 0, keepdims=False)

    following = lax.optimization_barrier(ahead(1))

    solved = jnp.zeros((share, width), BF16)
    previous = jnp.zeros((share, width), BF16)
    kept = jnp.zeros((panels - 4, share, width), BF16)
    arrivals = [[] for _ in range(panels)]

    def send(value, senders, distance):
        moved = lax.ppermute(value, "panel", [(s, s + distance) for s in senders])
        for s in senders:
            arrivals[s + distance].append(moved.astype(F32))

    for k in range(panels):
        earlier = sum(arrivals[k], jnp.zeros((share, width), F32))
        fresh = times((own_rhs - earlier).astype(BF16), inverse).astype(BF16)
        solved = jnp.where(z == k, fresh, solved)
        if k == panels - 1:
            break
        if k > 0:
            fresh, previous = lax.optimization_barrier((fresh, previous))
        near = times(fresh, following).astype(BF16)
        near, fresh = lax.optimization_barrier((near, fresh))
        send(near, [k], 1)
        if k < panels - 2:
            *after, kept = stage_products(z, k, fresh, previous, whole, kept)
            send(after[0], [k], 2)
        if k < panels - 3:
            send(after[1], [k], 3)
        previous = fresh
        for distance, senders in FAR_SENDS.get(k, ()):
            send(kept[distance - 4], senders, distance)
    mine = lax.all_to_all(
        jnp.broadcast_to(solved[None], (chips, share, width)), "chip", 0, 0, tiled=True
    )
    products = times(mine.reshape(-1, width), both_tall).astype(BF16)
    products = products.reshape(batches, -1, 2 * tall_rows)

    def part(batch):
        return lax.dynamic_index_in_dim(products, batch, 0, keepdims=False)

    summed = part(z).astype(F32)
    for distance in sorted(range(1, panels), key=lambda d: -abs(2 * d - panels)):
        route = [(s, (s + distance) % panels) for s in range(panels)]
        moved = lax.ppermute(part(lax.rem(z + distance, panels)), "panel", route)
        summed = summed + moved.astype(F32)

    def in_order(own, other):
        lead, rows = own.shape[:-2], own.shape[-1]
        own = own.reshape(*lead, -1, 1, share, rows)
        other = other.reshape(*lead, -1, 1, share, rows)
        sides = lax.broadcasted_iota(jnp.int32, (2, 1, 1), 0)
        whole_row = jnp.where(sides == core, own, other).reshape(*lead, columns, rows)
        return jnp.swapaxes(whole_row, -1, -2)

    def rows_of(index):
        rows = lax.dynamic_slice_in_dim(mine, index * slice_rows, slice_rows, 2)
        return rows.reshape(batches, -1, slice_rows)

    other_rows = swap(rows_of(rows_index + 1 - 2 * core))
    solution_rows = in_order(rows_of(rows_index), other_rows).astype(F32)

    tall_sum = in_order(summed[:, :tall_rows], swap(summed[:, tall_rows:]))
    return solution_rows[None], rhs_tall.astype(F32) - tall_sum[None]


def solution(mesh):
    panels, rows = mesh.devices.shape
    split = Mesh(mesh.devices.reshape(panels, rows // 2, 2), ("panel", "chip", "core"))
    placed = (
        P(None, ROWS, None),
        P("panel", ROWS, None),
        P("panel", None, None),
        P("panel", ROWS, None),
        P("panel", ROWS, None, None),
        P(ROWS, "panel"),
    )
    return jax.shard_map(
        per_device,
        mesh=split,
        in_specs=placed,
        out_specs=(P("panel", None, ROWS, None), P("panel", ROWS, None)),
        check_vma=False,
    )
```
